256 devices in a mesh: leaf: 8 (over y, core), node: 32 (over z, x).
Axes of the slice: x: 4, y: 4, z: 8, core: 2. Of those that a mesh axis runs over, the one named last changes fastest.
Arguments:
- sources: bfloat16 [2048, 131072], P('node', 'leaf'), may hold values from -6 to 6
- block_inverse: bfloat16 [512, 131072], P(None, ('leaf', 'node')), may hold values from -0.25 to 0.25
- basis_left: bfloat16 [64, 131072], P(None, ('leaf', 'node')), may hold values from -0.046875 to 0.046875
- basis_right: bfloat16 [64, 131072], P(None, ('leaf', 'node')), may hold values from -0.75 to 0.75
- couple_in: bfloat16 [64, 131072], P(None, ('leaf', 'node')), may hold values from -0.046875 to 0.046875
- couple_out: bfloat16 [64, 131072], P(None, ('leaf', 'node')), may hold values from -0.5 to 0.5
- column_of_shot: int32 [2048], replicated, may hold values from 0 to 2047, each once
- cell_map: int32 [131072], P(('leaf', 'node')), may hold values from 0 to 65535
Outputs:
- solution: bfloat16 [2048, 131072], P(None, ('leaf', 'node'))
- gradient: float32 [65536], P('node')
The draws below stay inside these ranges and needn't reach their ends.
Inputs may be any that keep to these rules, and one draw needn't show every extreme that they name: `column_of_shot`: a permutation of the 2048 column numbers.
All inputs are finite; a program needn't handle non-finite values.
Results may differ from the reference program's by a relative error of at most 0.02.
Values may be sent and summed in bfloat16 or wider, within the bound.
No kernel may reach another device: no remote copies, remote signals or barrier semaphores. Data moves between devices by JAX's collectives and lax.ppermute only.
A program may use at most 64 MiB of HBM per device.

```python
import jax
import jax.numpy as jnp
from jax import lax

BLOCK = 512
K = 64
NCOL = 2048
FRONT = 16384
ROWS = 131072
CELLS = 65536
N_LEAF = 8


def touch_ends(result, key, least, largest):
    dims = result.shape
    place = [jax.random.randint(jax.random.fold_in(key, axis), (), 0, dims[axis]) for axis in range(len(dims))]
    result = result.at[tuple(place)].set(least)
    longest = dims.index(max(dims))
    place[longest] = (place[longest] + 1) % dims[longest]
    return result.at[tuple(place)].set(largest)


def steps_of(key, dims, split, low, largest):
    gain = 1.0
    for position, parts in split:
        steps = jax.random.uniform(jax.random.fold_in(jax.random.fold_in(key, 6), position), (parts,), jnp.float32, low / len(split), largest / len(split))
        gain = gain * jnp.repeat(jnp.exp(steps), dims[position] // parts).reshape((-1,) + (1,) * (len(dims) - 1 - position))
    return gain


def centred(stream_key, shape, width, limit, pieces=(), kind=jnp.bfloat16):
    drawn = jax.random.normal(stream_key, shape, jnp.float32) * width
    if len(pieces) > 0:
        drawn = steps_of(stream_key, shape, pieces, -0.22, 0.18) * drawn
    return jnp.clip(drawn, min=-limit, max=limit).astype(kind)


def setup_inputs(seed: int = 0) -> dict:
    streams_of = jax.random.split(jax.random.key(seed), 9)
    return {
        "sources": centred(streams_of[0], (NCOL, ROWS), 1.0, 6.0, ((0, 32), (1, 8))),
        "block_inverse": centred(streams_of[1], (BLOCK, ROWS), BLOCK ** -0.5, 0.25, ((1, 256),)),
        "basis_left": centred(streams_of[2], (K, ROWS), FRONT ** -0.5, 0.046875, ((1, 256),)),
        "basis_right": centred(streams_of[3], (K, ROWS), K ** -0.5, 0.75, ((1, 256),)),
        "couple_in": centred(streams_of[4], (K, ROWS), FRONT ** -0.5, 0.046875, ((1, 256),)),
        "couple_out": centred(streams_of[5], (K, ROWS), 0.08, 0.5, ((1, 256),)),
        "column_of_shot": jax.random.permutation(streams_of[6], NCOL).astype(jnp.int32),
        "cell_map": touch_ends(jax.random.randint(streams_of[7], (ROWS,), 0, CELLS), jax.random.fold_in(streams_of[7], 1), 0, CELLS - 1).astype(jnp.int32),
    }


def apply_group(values, inverse_blocks, left_basis, right_basis, transposed):
    count = values.shape[0]
    value_blocks = values.reshape(count, -1, BLOCK).astype(jnp.float32)
    matrix_blocks = inverse_blocks.reshape(BLOCK, -1, BLOCK).astype(jnp.float32)
    if transposed:
        local_part = jnp.einsum('rmi,jmi->rmj', value_blocks, matrix_blocks, precision=lax.Precision.HIGHEST)
    else:
        local_part = jnp.einsum('rmi,imj->rmj', value_blocks, matrix_blocks, precision=lax.Precision.HIGHEST)
    local_part = local_part.reshape(count, -1)
    projected = jnp.dot(values, left_basis.T, preferred_element_type=jnp.float32).astype(jnp.bfloat16)
    return (local_part + jnp.dot(projected, right_basis, preferred_element_type=jnp.float32)).astype(jnp.bfloat16)

def reference(sources, block_inverse, basis_left, basis_right, couple_in, couple_out, column_of_shot, cell_map):
    inverse = jnp.zeros((NCOL,), jnp.int32).at[column_of_shot].set(jnp.arange(NCOL, dtype=jnp.int32))
    rhs_cols = sources[inverse]
    incoming = jnp.zeros((NCOL, K), jnp.float32)
    forwards = []
    for group in range(N_LEAF):
        window = slice(group * FRONT, (group + 1) * FRONT)
        fwd_rhs = apply_group(rhs_cols[:, window], block_inverse[:, window], basis_left[:, window], basis_right[:, window], False)
        fwd_couple = apply_group(couple_in[:, window], block_inverse[:, window], basis_left[:, window], basis_right[:, window], False)
        carry = jnp.dot(fwd_rhs, couple_out[:, window].T, preferred_element_type=jnp.float32)
        step_map = -jnp.dot(fwd_couple, couple_out[:, window].T, preferred_element_type=jnp.float32)
        forward = fwd_rhs.astype(jnp.float32) - jnp.dot(incoming, fwd_couple.astype(jnp.float32), precision=lax.Precision.HIGHEST)
        forwards.append(forward.astype(jnp.bfloat16))
        incoming = carry + jnp.dot(incoming, step_map, precision=lax.Precision.HIGHEST)
    returning = jnp.zeros((NCOL, K), jnp.float32)
    solutions = [None] * N_LEAF
    for group in range(N_LEAF - 1, -1, -1):
        window = slice(group * FRONT, (group + 1) * FRONT)
        back_rhs = apply_group(forwards[group], block_inverse[:, window], basis_right[:, window], basis_left[:, window], True)
        back_couple = apply_group(couple_out[:, window], block_inverse[:, window], basis_right[:, window], basis_left[:, window], True)
        lift = jnp.dot(back_rhs, couple_in[:, window].T, preferred_element_type=jnp.float32)
        turn_map = -jnp.dot(back_couple, couple_in[:, window].T, preferred_element_type=jnp.float32)
        solved = back_rhs.astype(jnp.float32) - jnp.dot(returning, back_couple.astype(jnp.float32), precision=lax.Precision.HIGHEST)
        solutions[group] = solved.astype(jnp.bfloat16)
        returning = lift + jnp.dot(returning, turn_map, precision=lax.Precision.HIGHEST)
    solution = jnp.concatenate(solutions, axis=1)
    forward_all = jnp.concatenate(forwards, axis=1)
    corr = lax.optimization_barrier(jnp.sum(solution.astype(jnp.float32) * forward_all.astype(jnp.float32), axis=0)) / jnp.sqrt(jnp.float32(NCOL))
    gradient = jnp.zeros((CELLS,), jnp.float32).at[cell_map].add(corr)
    return (solution, gradient)
```

```python
import functools

import jax
import jax.numpy as jnp
from jax import lax
from jax.experimental import pallas as pl
from jax.experimental.pallas import tpu as pltpu
from jax.sharding import Mesh, PartitionSpec as P

BLOCK = 512
RANK = 64
NZ = 8
NX = 4
NLEAF = 8
LANES = 128
BF = jnp.bfloat16
F32 = jnp.float32
NT = (((1,), (1,)), ((), ()))
VMEM_SPEC = pl.BlockSpec(memory_space=pltpu.VMEM)
SMEM_SPEC = pl.BlockSpec(memory_space=pltpu.SMEM)


def dot(a, b):
    return jnp.dot(a.astype(BF), b.astype(BF), preferred_element_type=F32)


def dot_nt(a, b):
    return lax.dot_general(a.astype(BF), b.astype(BF), NT, preferred_element_type=F32)


def prepare_kernel(d_ref, left_ref, right_ref, cin_ref, cout_ref, w_ref, g_ref, re_ref, lc_ref):
    d = d_ref[...]
    left = left_ref[...]
    right = right_ref[...]
    cin = cin_ref[...]
    both = jnp.concatenate([cout_ref[...], right], axis=0)
    cin_d = dot(cin, d)
    both_dt = dot_nt(both, d)
    w_ref[0:64, :] = left
    w_ref[64:192, :] = both_dt.astype(BF)
    w_ref[192:256, :] = dot_nt(cin_d, d).astype(BF)
    g_ref[:, 0:256] = dot_nt(cin, w_ref[...])
    g_ref[:, 256:384] = dot_nt(right, both)
    re_ref[0:64, :] = right
    re_ref[64:128, :] = (-cin_d).astype(BF)
    lc_ref[0:64, :] = left
    lc_ref[64:128, :] = (-both_dt[0:64, :]).astype(BF)


def prepare(d, left, right, cin, cout):
    return pl.pallas_call(
        prepare_kernel,
        name="prepare",
        out_shape=(
            jax.ShapeDtypeStruct((4 * RANK, BLOCK), BF),
            jax.ShapeDtypeStruct((RANK, 6 * RANK), F32),
            jax.ShapeDtypeStruct((2 * RANK, BLOCK), BF),
            jax.ShapeDtypeStruct((2 * RANK, BLOCK), BF),
        ),
        in_specs=[VMEM_SPEC] * 5,
        out_specs=(VMEM_SPEC,) * 4,
    )(d, left, right, cin, cout)


def project_kernel(x_ref, v_ref, w0, w1, w2, w3, y_ref, p0, p1, p2, p3):
    x = x_ref[0]
    total = None
    for k, w in enumerate((w0, w1, w2, w3)):
        at = pl.multiple_of(lax.rem(x + (NX - k), NX) * BLOCK, BLOCK)
        part = lax.dot_general(v_ref[:, pl.ds(at, BLOCK)], w[...], NT, preferred_element_type=F32)
        total = part if total is None else total + part
    y_ref[...] = total.astype(BF)
    for k, piece in enumerate((p0, p1, p2, p3)):
        at = pl.multiple_of(lax.rem(x + k, NX) * BLOCK, BLOCK)
        piece[...] = v_ref[:, pl.ds(at, BLOCK)]


def project(x, v, ws):
    rows = v.shape[0]
    return pl.pallas_call(
        project_kernel,
        name="project",
        out_shape=(jax.ShapeDtypeStruct((rows, 4 * RANK), BF),)
        + (jax.ShapeDtypeStruct((rows, BLOCK), BF),) * NX,
        in_specs=[SMEM_SPEC] + [VMEM_SPEC] * 5,
        out_specs=(VMEM_SPEC,) * 5,
    )(x, v, *ws)


def recur_kernel(at_ref, y_ref, g_ref, out_ref):
    mine = at_ref[0]
    cols = lambda a, i: a[:, i * RANK : (i + 1) * RANK]
    zero = jnp.zeros((y_ref.shape[1], RANK), F32)
    inc = zero
    held = [zero] * 4
    p_mine = m1_mine = jnp.zeros((RANK, RANK), F32)
    steps, lifts = [], []
    pick = lambda j, new, old: jnp.where(mine == j, new, old)
    for j in range(NLEAF):
        maps = g_ref[at_ref[1 + j]]
        p, s1, s2, s4, m1, m2 = (cols(maps, i) for i in range(6))
        y = y_ref[j].astype(F32)
        proj, y_carry, y_q, y_lift = (cols(y, i) for i in range(4))
        step = -(s1 + dot(p, m1))
        q_map = s2 + dot(p, m2)
        lift_map = s4 + dot_nt(p, s2)
        q = y_q + dot(proj, m2) - dot(inc, q_map)
        lift = y_lift + dot_nt(proj, s2) - dot(inc, lift_map) + dot_nt(q, p)
        held = [pick(j, a, b) for a, b in zip((proj, inc, q, zero), held)]
        p_mine = pick(j, p, p_mine)
        m1_mine = pick(j, m1, m1_mine)
        inc = y_carry + dot(proj, m1) + dot(inc, step)
        steps.append(step)
        lifts.append(lift)
    ret = zero
    ret_mine = zero
    for j in range(NLEAF - 1, -1, -1):
        ret_mine = pick(j, ret, ret_mine)
        if j:
            ret = lifts[j] + dot_nt(ret, steps[j])
    proj, inc, q = held[:3]
    out_ref[:, 0:64] = (proj - dot(inc, p_mine)).astype(BF)
    out_ref[:, 64:128] = inc.astype(BF)
    out_ref[:, 128:192] = (q - dot_nt(ret_mine, m1_mine)).astype(BF)
    out_ref[:, 192:256] = ret_mine.astype(BF)


def recur(at, y, g):
    return pl.pallas_call(
        recur_kernel,
        name="recur",
        out_shape=jax.ShapeDtypeStruct(y.shape[1:], BF),
        in_specs=[SMEM_SPEC, VMEM_SPEC, VMEM_SPEC],
        out_specs=VMEM_SPEC,
    )(at, y, g)


def finish_kernel(x_ref, v0, v1, v2, v3, c_ref, d_ref, re_ref, lc_ref, map_ref, sol_ref, cell_ref):
    x = x_ref[0]
    rows = v0.shape[0]
    corr = jnp.zeros((1, BLOCK), F32)
    for k, v in enumerate((v0, v1, v2, v3)):
        node = lax.rem(x + (NX - k), NX)
        coef = c_ref[:, node].reshape(rows, 4 * RANK)
        fwd = dot(v[...], d_ref[...]) + dot(coef[:, 0:128], re_ref[...])
        fwd = fwd.astype(BF)
        sol = dot_nt(fwd, d_ref[...]) + dot(coef[:, 128:256], lc_ref[...])
        sol = sol.astype(BF)
        sol_ref[pl.ds(k * rows, rows), :] = sol
        corr += jnp.sum(sol.astype(F32) * fwd.astype(F32), axis=0, keepdims=True)
    corr = corr * (1.0 / jnp.sqrt(F32(NX * rows)))
    cell = map_ref[...]
    count = cell_ref.shape[0]
    high = lax.broadcasted_iota(jnp.int32, (count, BLOCK), 0) == cell // LANES
    low = lax.broadcasted_iota(jnp.int32, (LANES, BLOCK), 0) == cell % LANES
    hot = jnp.where(low, 1.0, 0.0).astype(BF)
    first = corr.astype(BF).astype(F32)
    cells = dot_nt(jnp.where(high, first, 0.0), hot) + dot_nt(jnp.where(high, corr - first, 0.0), hot)
    cell_ref[...] = cells.astype(BF)


def finish(x, vs, coef, d, re, lc, cells, cell_rows):
    rows = vs[0].shape[0]
    return pl.pallas_call(
        finish_kernel,
        name="finish",
        out_shape=(
            jax.ShapeDtypeStruct((NX * rows, BLOCK), BF),
            jax.ShapeDtypeStruct((cell_rows, LANES), BF),
        ),
        in_specs=[SMEM_SPEC] + [VMEM_SPEC] * 9,
        out_specs=(VMEM_SPEC,) * 2,
    )(x, *vs, coef, d, re, lc, cells)


def shifted(a, axis, by):
    count = lax.axis_size(axis)
    return lax.ppermute(a, axis, [(i, (i + by) % count) for i in range(count)])


def swapped(a, axis, bit):
    return lax.ppermute(a, axis, [(i, i ^ bit) for i in range(lax.axis_size(axis))])


def broadcast(a, axes):
    count = lax.axis_size(axes)
    return lax.all_to_all(jnp.broadcast_to(a[None], (count, *a.shape)), axes, 0, 0, tiled=True)


def per_device(
    sources, block_inverse, basis_left, basis_right, couple_in, couple_out, column_of_shot, cell_map
):
    node = ("z", "x")
    shots = sources.shape[0]
    z, x, leaf = (lax.axis_index(a) for a in ("z", "x", "leaf"))
    y, core = leaf // 2, leaf % 2
    with jax.named_scope("move_z"):
        by_z = jnp.swapaxes(sources.reshape(shots, NZ, NX * BLOCK), 0, 1)
        v = lax.all_to_all(by_z, "z", 0, 0, tiled=True).reshape(NZ * shots, NX * BLOCK)
    w, g, re, lc = prepare(block_inverse, basis_left, basis_right, couple_in, couple_out)
    with jax.named_scope("maps"):
        ws = [w] + [shifted(w, "x", k) for k in range(1, NX)]
        for axis, bit in (("x", 1), ("x", 2), ("z", 1), ("z", 2), ("z", 4)):
            g = g + swapped(g, axis, bit)
        pair = jnp.stack([g, swapped(g, "leaf", 1)])
        far = [pair] + [shifted(pair, "leaf", 2 * k) for k in range(1, NLEAF // 2)]
        maps = jnp.concatenate(far, axis=0)
    here = x.reshape(1).astype(jnp.int32)
    part, *pieces = project(here, v, ws)
    with jax.named_scope("move_x"):
        vs = [pieces[0]] + [shifted(pieces[k], "x", k) for k in range(1, NX)]
    with jax.named_scope("sum_z"):
        own = lax.all_to_all(part.reshape(NZ, shots, 4 * RANK), "z", 0, 0, tiled=True)
        own = own.astype(F32).sum(axis=0).astype(BF)
    with jax.named_scope("over_leaf"):
        every = broadcast(own, "leaf")
    group = jnp.arange(NLEAF, dtype=jnp.int32)
    place = ((y - group // 2) % (NLEAF // 2)) * 2 + (group % 2 + core) % 2
    at = jnp.concatenate([leaf.reshape(1), place]).astype(jnp.int32)
    coef = recur(at, every, maps)
    with jax.named_scope("over_node"):
        coef = broadcast(coef, node).reshape(NZ, NX, shots, 4 * RANK)
    cell_rows = NZ * NX * 2048 // LANES
    sol, cells = finish(
        here, vs, coef, block_inverse, re, lc, cell_map.reshape(1, BLOCK), cell_rows
    )
    with jax.named_scope("cells"):
        parts = cells.reshape(NZ * NX, cell_rows // (NZ * NX), LANES)
        parts = lax.all_to_all(parts, node, 0, 0, tiled=True)
        slab = parts.astype(F32).sum(axis=0)
        gradient = broadcast(slab, "leaf").sum(axis=0).reshape(-1)
    with jax.named_scope("columns"):
        shot = jnp.arange(NZ * NX * shots, dtype=jnp.int32)
        from_node = shot // shots
        row = ((x - from_node % NX) % NX) * (NZ * shots) + (from_node // NX) * shots + shot % shots
        source_row = jnp.zeros_like(row).at[column_of_shot].set(row)
        solution = jnp.take(sol, source_row, axis=0)
    return solution, gradient


def solution(mesh):
    split = Mesh(mesh.devices.reshape(NLEAF, NZ, NX), ("leaf", "z", "x"))
    block = P(None, ("leaf", "z", "x"))
    return jax.shard_map(
        per_device,
        mesh=split,
        in_specs=(
            P(("z", "x"), "leaf"),
            block,
            block,
            block,
            block,
            block,
            P(),
            P(("leaf", "z", "x")),
        ),
        out_specs=(block, P(("z", "x"))),
        check_vma=False,
    )
```

```python
import jax
import jax.numpy as jnp
from jax import lax
from jax.experimental import pallas as pl
from jax.experimental.pallas import tpu as pltpu
from jax.sharding import Mesh, PartitionSpec as P


BLOCK = 512
RANK = 64
NZ = 8
NX = 4
NLEAF = 8
LANES = 128
BF = jnp.bfloat16
F32 = jnp.float32
NT = (((1,), (1,)), ((), ()))
VMEM_SPEC = pl.BlockSpec(memory_space=pltpu.VMEM)
SMEM_SPEC = pl.BlockSpec(memory_space=pltpu.SMEM)


def dot(a, b):
    return jnp.dot(a.astype(BF), b.astype(BF), preferred_element_type=F32)


def dot_nt(a, b):
    return lax.dot_general(a.astype(BF), b.astype(BF), NT, preferred_element_type=F32)


def prepare_kernel(d_ref, left_ref, right_ref, cin_ref, cout_ref, w_ref, g_ref, back_ref):
    d = d_ref[...]
    right = right_ref[...]
    cin = cin_ref[...]
    both = jnp.concatenate([right, cout_ref[...]], axis=0)
    cin_d = dot(cin, d)
    w_ref[0:64, :] = left_ref[...]
    w_ref[64:192, :] = dot_nt(both, d).astype(BF)
    w_ref[192:256, :] = dot_nt(cin_d, d).astype(BF)
    g_ref[:, 0:256] = dot_nt(cin, w_ref[...])
    g_ref[:, 256:384] = dot_nt(right, both)
    back_ref[...] = cin_d.astype(BF)


def prepare(d, left, right, cin, cout):
    return pl.pallas_call(
        prepare_kernel,
        name="prepare",
        out_shape=(
            jax.ShapeDtypeStruct((4 * RANK, BLOCK), BF),
            jax.ShapeDtypeStruct((RANK, 6 * RANK), F32),
            jax.ShapeDtypeStruct((RANK, BLOCK), BF),
        ),
        in_specs=[VMEM_SPEC] * 5,
        out_specs=(VMEM_SPEC,) * 3,
    )(d, left, right, cin, cout)


def project_kernel(x_ref, v_ref, w0, w1, w2, w3, g_ref, y_ref, p0, p1, p2, p3, g_out):
    x = x_ref[0]
    total = None
    for k, w in enumerate((w0, w1, w2, w3)):
        at = pl.multiple_of(lax.rem(x + (NX - k), NX) * BLOCK, BLOCK)
        part = lax.dot_general(v_ref[:, pl.ds(at, BLOCK)], w[...], NT, preferred_element_type=F32)
        total = part if total is None else total + part
    y_ref[...] = total.astype(BF)
    for k, piece in enumerate((p0, p1, p2, p3)):
        at = pl.multiple_of(lax.rem(x + k, NX) * BLOCK, BLOCK)
        piece[...] = v_ref[:, pl.ds(at, BLOCK)]
    g_out[...] = g_ref[...]


def project(x, v, ws, g):
    rows = v.shape[0]
    return pl.pallas_call(
        project_kernel,
        name="project",
        out_shape=(jax.ShapeDtypeStruct((rows, 4 * RANK), BF),)
        + (jax.ShapeDtypeStruct((rows, BLOCK), BF),) * NX
        + (jax.ShapeDtypeStruct(g.shape, g.dtype),),
        in_specs=[SMEM_SPEC] + [VMEM_SPEC] * 6,
        out_specs=(VMEM_SPEC,) * 6,
    )(x, v, *ws, g)


def total_kernel(part_ref, own_ref, early_ref):
    own = part_ref[0].astype(F32)
    for i in range(1, NZ):
        own += part_ref[i].astype(F32)
    own = own.astype(BF)
    own_ref[...] = own
    for i in range(NZ * NX):
        early_ref[i] = own[:, 0:128]


def total(parts):
    shots = parts.shape[1]
    return pl.pallas_call(
        total_kernel,
        name="total",
        out_shape=(
            jax.ShapeDtypeStruct((shots, 4 * RANK), BF),
            jax.ShapeDtypeStruct((NZ * NX, shots, 2 * RANK), BF),
        ),
        in_specs=[VMEM_SPEC],
        out_specs=(VMEM_SPEC,) * 2,
    )(parts)


def cols(a, i):
    return a[:, i * RANK : (i + 1) * RANK]


def lowrank_kernel(g_ref, d_ref, left_ref, right_ref, cin_d_ref, cout_ref, wf_ref, ws_ref):
    p, s2, _, _, m2, m1 = (cols(g_ref[...], i) for i in range(6))
    left = left_ref[...]
    right = right_ref[...]
    zero = jnp.zeros((RANK, BLOCK), BF)
    wf_ref[0:64, :] = right
    wf_ref[64:128, :] = zero
    wf_ref[128:192, :] = (-(cin_d_ref[...].astype(F32) + dot(p, right))).astype(BF)
    wf_ref[192:256, :] = zero
    ws_ref[0:64, :] = dot(m2, left).astype(BF)
    ws_ref[64:128, :] = left
    ws_ref[128:192, :] = (-dot(s2 + dot(p, m2), left)).astype(BF)
    ws_ref[192:256, :] = (-(dot_nt(cout_ref[...], d_ref[...]) + dot(m1.T, left))).astype(BF)


def lowrank(g, d, left, right, cin_d, cout):
    return pl.pallas_call(
        lowrank_kernel,
        name="lowrank",
        out_shape=(jax.ShapeDtypeStruct((4 * RANK, BLOCK), BF),) * 2,
        in_specs=[VMEM_SPEC] * 6,
        out_specs=(VMEM_SPEC,) * 2,
    )(g, d, left, right, cin_d, cout)


def recur_kernel(at_ref, f0, f1, f2, f3, out_ref, all_ref):
    for k, f in enumerate((f0, f1, f2, f3)):
        all_ref[pl.ds(2 * k, 2)] = f[...]
    mine = at_ref[0]
    zero = jnp.zeros((f0.shape[1], RANK), F32)
    inc = inc_mine = zero
    steps, lifts = [], []
    for j in range(NLEAF):
        both = all_ref[at_ref[1 + j]]
        maps = both[:, 256:640].astype(F32)
        p, s2, s1, s4, m2, m1 = (cols(maps, i) for i in range(6))
        y = both[:, 0:256].astype(F32)
        proj, y_q, y_carry, y_lift = (cols(y, i) for i in range(4))
        step = -(s1 + dot(p, m1))
        q_map = s2 + dot(p, m2)
        lift_map = s4 + dot_nt(p, s2)
        q = y_q + dot(proj, m2) - dot(inc, q_map)
        lift = y_lift + dot_nt(proj, s2) - dot(inc, lift_map) + dot_nt(q, p)
        inc_mine = jnp.where(mine == j, inc, inc_mine)
        inc = y_carry + dot(proj, m1) + dot(inc, step)
        steps.append(step)
        lifts.append(lift)
    ret = ret_mine = zero
    for j in range(NLEAF - 1, -1, -1):
        ret_mine = jnp.where(mine == j, ret, ret_mine)
        if j:
            ret = lifts[j] + dot_nt(ret, steps[j])
    late = jnp.concatenate([inc_mine, ret_mine], axis=1).astype(BF)
    for i in range(NZ * NX):
        out_ref[i] = late


def recur(at, far):
    shots = far[0].shape[1]
    return pl.pallas_call(
        recur_kernel,
        name="recur",
        out_shape=jax.ShapeDtypeStruct((NZ * NX, shots, 2 * RANK), BF),
        in_specs=[SMEM_SPEC] + [VMEM_SPEC] * 4,
        out_specs=VMEM_SPEC,
        scratch_shapes=[pltpu.VMEM((NLEAF, *far[0].shape[1:]), BF)],
    )(at, *far)


def finish_kernel(
    x_ref, v0, v1, v2, v3, early_ref, late_ref, d_ref, wf_ref, ws_ref, map_ref, sol_ref, cell_ref
):
    x = x_ref[0]
    rows = v0.shape[0]
    corr = jnp.zeros((1, BLOCK), F32)
    for k, v in enumerate((v0, v1, v2, v3)):
        node = lax.rem(x + (NX - k), NX)
        coef = jnp.concatenate(
            [r[:, node].reshape(rows, 2 * RANK) for r in (early_ref, late_ref)], axis=1
        )
        fwd = dot(v[...], d_ref[...]) + dot(coef, wf_ref[...])
        fwd = fwd.astype(BF)
        sol = dot_nt(fwd, d_ref[...]) + dot(coef, ws_ref[...])
        sol = sol.astype(BF)
        sol_ref[pl.ds(k * rows, rows), :] = sol
        corr += jnp.sum(sol.astype(F32) * fwd.astype(F32), axis=0, keepdims=True)
    corr = corr * (1.0 / jnp.sqrt(F32(NX * rows)))
    cell = map_ref[...]
    count = cell_ref.shape[0]
    high = lax.broadcasted_iota(jnp.int32, (count, BLOCK), 0) == cell // LANES
    low = lax.broadcasted_iota(jnp.int32, (LANES, BLOCK), 0) == cell % LANES
    hot = jnp.where(low, 1.0, 0.0).astype(BF)
    first = corr.astype(BF).astype(F32)
    cells = dot_nt(jnp.where(high, first, 0.0), hot) + dot_nt(jnp.where(high, corr - first, 0.0), hot)
    cell_ref[...] = cells.astype(BF)


def finish(x, vs, early, late, d, wf, ws, cells, cell_rows):
    rows = vs[0].shape[0]
    return pl.pallas_call(
        finish_kernel,
        name="finish",
        out_shape=(
            jax.ShapeDtypeStruct((NX * rows, BLOCK), BF),
            jax.ShapeDtypeStruct((cell_rows, LANES), BF),
        ),
        in_specs=[SMEM_SPEC] + [VMEM_SPEC] * 10,
        out_specs=(VMEM_SPEC,) * 2,
    )(x, *vs, early, late, d, wf, ws, cells)


def shifted(a, axis, by):
    count = lax.axis_size(axis)
    return lax.ppermute(a, axis, [(i, (i + by) % count) for i in range(count)])


def swapped(a, axis, bit):
    return lax.ppermute(a, axis, [(i, i ^ bit) for i in range(lax.axis_size(axis))])


def broadcast(a, axes):
    count = lax.axis_size(axes)
    return lax.all_to_all(jnp.broadcast_to(a[None], (count, *a.shape)), axes, 0, 0, tiled=True)


def per_device(
    sources, block_inverse, basis_left, basis_right, couple_in, couple_out, column_of_shot, cell_map
):
    node = ("z", "x")
    shots = sources.shape[0]
    _, x, leaf = (lax.axis_index(a) for a in ("z", "x", "leaf"))
    y, core = leaf // 2, leaf % 2
    by_z = jnp.swapaxes(sources.reshape(shots, NZ, NX * BLOCK), 0, 1)
    v = lax.all_to_all(by_z, "z", 0, 0, tiled=True).reshape(NZ * shots, NX * BLOCK)
    w, g, cin_d = prepare(block_inverse, basis_left, basis_right, couple_in, couple_out)
    ws = [w] + [shifted(w, "x", k) for k in range(1, NX)]
    for bit in (1, 2):
        g = g + swapped(g, "x", bit)
    here = x.reshape(1).astype(jnp.int32)
    part, *pieces, g = project(here, v, ws, g)
    parts = lax.all_to_all(part.reshape(NZ, shots, 4 * RANK), "z", 0, 0, tiled=True)
    vs = [pieces[0]] + [shifted(pieces[k], "x", k) for k in range(1, NX)]
    for bit in (1, 2, 4):
        g = g + swapped(g, "z", bit)
    wf, ws = lowrank(g, block_inverse, basis_left, basis_right, cin_d, couple_out)
    own, early = total(parts)
    early = lax.all_to_all(early, node, 0, 0, tiled=True)
    own = jnp.concatenate([own, g.astype(BF)], axis=1)
    pair = jnp.stack([own, swapped(own, "leaf", 1)])
    far = [pair] + [shifted(pair, "leaf", 2 * k) for k in range(1, NLEAF // 2)]
    group = jnp.arange(NLEAF, dtype=jnp.int32)
    place = ((y - group // 2) % (NLEAF // 2)) * 2 + (group % 2 + core) % 2
    at = jnp.concatenate([leaf.reshape(1), place]).astype(jnp.int32)
    late = recur(at, far)
    late = lax.all_to_all(late, node, 0, 0, tiled=True)
    early, late = (a.reshape(NZ, NX, shots, 2 * RANK) for a in (early, late))
    cell_rows = NZ * NX * 2048 // LANES
    sol, cells = finish(
        here, vs, early, late, block_inverse, wf, ws, cell_map.reshape(1, BLOCK), cell_rows
    )
    parts = cells.reshape(NZ * NX, cell_rows // (NZ * NX), LANES)
    parts = lax.all_to_all(parts, node, 0, 0, tiled=True)
    slab = parts.astype(F32).sum(axis=0)
    gradient = broadcast(slab, "leaf").sum(axis=0).reshape(-1)
    shot = jnp.arange(NZ * NX * shots, dtype=jnp.int32)
    from_node = shot // shots
    row = ((x - from_node % NX) % NX) * (NZ * shots) + (from_node // NX) * shots + shot % shots
    source_row = jnp.zeros_like(row).at[column_of_shot].set(row)
    solution = jnp.take(sol, source_row, axis=0)
    return solution, gradient


def solution(mesh):
    split = Mesh(mesh.devices.reshape(NLEAF, NZ, NX), ("leaf", "z", "x"))
    block = P(None, ("leaf", "z", "x"))
    return jax.shard_map(
        per_device,
        mesh=split,
        in_specs=(
            P(("z", "x"), "leaf"),
            block,
            block,
            block,
            block,
            block,
            P(),
            P(("leaf", "z", "x")),
        ),
        out_specs=(block, P(("z", "x"))),
        check_vma=False,
    )
```

```python
import functools

import jax
import jax.numpy as jnp
from jax import lax
from jax.experimental import pallas as pl
from jax.experimental.pallas import tpu as pltpu
from jax.sharding import Mesh, PartitionSpec as P


BLOCK = 512
RANK = 64
NZ = 8
NX = 4
NLEAF = 8
LANES = 128
SLAB = 2048
PACK = BLOCK + 2 * RANK + 16
BF = jnp.bfloat16
F32 = jnp.float32
NT = (((1,), (1,)), ((), ()))
VMEM_SPEC = pl.BlockSpec(memory_space=pltpu.VMEM)
SMEM_SPEC = pl.BlockSpec(memory_space=pltpu.SMEM)
ANY_SPEC = pl.BlockSpec(memory_space=pl.ANY)


def shaped(*shape, dtype=BF):
    return jax.ShapeDtypeStruct(shape, dtype)


def near(*arrays):
    return [pltpu.with_memory_space_constraint(a, pltpu.VMEM) for a in arrays]


def dot(a, b):
    return jnp.dot(a.astype(BF), b.astype(BF), preferred_element_type=F32)


def dot_nt(a, b):
    return lax.dot_general(a.astype(BF), b.astype(BF), NT, preferred_element_type=F32)


def cols(a, i):
    return a[:, i * RANK : (i + 1) * RANK]


def back(axis, by, count):
    return lax.rem(lax.axis_index(axis) + (count - by), count)


def prepare_kernel(s_ref, d_ref, left_ref, right_ref, cin_ref, cout_ref, map_ref, *refs):
    w_ref, g_ref, gb_ref, pack_ref = refs[:4]
    outs, (held, came, went) = refs[4 : 4 + NZ], refs[4 + NZ :]
    z = lax.axis_index("z")
    into, out = [], []
    for k in range(NZ):
        at = pl.multiple_of(lax.rem(z + k, NZ) * (NX * BLOCK), NX * BLOCK)
        source = s_ref.at[:, pl.ds(at, NX * BLOCK)]
        into.append(pltpu.make_async_copy(source, held.at[k], came.at[k]))
        out.append(pltpu.make_async_copy(held.at[k], outs[k], went.at[k]))
    for c in into:
        c.start()
    d = d_ref[...]
    right = right_ref[...]
    cin = cin_ref[...]
    both = jnp.concatenate([right, cout_ref[...]], axis=0)
    cin_d = dot(cin, d).astype(BF)
    for a, b in zip(into, out):
        a.wait()
        b.start()
    w_ref[0:64, :] = left_ref[...]
    w_ref[64:192, :] = dot_nt(both, d).astype(BF)
    w_ref[192:256, :] = dot_nt(cin_d, d).astype(BF)
    g_ref[:, 0:256] = dot_nt(cin, w_ref[...])
    g_ref[:, 256:384] = dot_nt(right, both)
    gb_ref[...] = g_ref[...].astype(BF)
    pack_ref[0:512, :] = d
    pack_ref[512:576, :] = right
    pack_ref[576:640, :] = cin_d
    cell = jnp.broadcast_to(map_ref[...], (16, BLOCK))
    upper = lax.broadcasted_iota(jnp.int32, cell.shape, 0) < 8
    pack_ref[640:656, :] = jnp.where(upper, cell // (2 * LANES), cell % (2 * LANES)).astype(F32).astype(BF)
    for c in out:
        c.wait()


def prepare(sources, *args):
    part = (sources.shape[0], NX * BLOCK)
    return pl.pallas_call(
        prepare_kernel,
        name="prepare",
        out_shape=(
            shaped(4 * RANK, BLOCK),
            shaped(RANK, 6 * RANK, dtype=F32),
            shaped(RANK, 6 * RANK),
            shaped(PACK, BLOCK),
        )
        + (shaped(*part),) * NZ,
        in_specs=[ANY_SPEC] + [VMEM_SPEC] * 6,
        out_specs=(VMEM_SPEC,) * 4 + (ANY_SPEC,) * NZ,
        scratch_shapes=[
            pltpu.VMEM((NZ, *part), BF),
            pltpu.SemaphoreType.DMA((NZ,)),
            pltpu.SemaphoreType.DMA((NZ,)),
        ],
    )(sources, *args)


def blocks_into(vs, k, v_ref):
    at = pl.multiple_of(back("x", k, NX) * BLOCK, BLOCK)
    shots = vs[0].shape[0]
    return [
        (v.at[:, pl.ds(at, BLOCK)], v_ref.at[k, pl.ds(i * shots, shots)]) for i, v in enumerate(vs)
    ]


def block_of(vs, k):
    at = pl.multiple_of(back("x", k, NX) * BLOCK, BLOCK)
    return jnp.concatenate([v[:, pl.ds(at, BLOCK)] for v in vs], axis=0)


def project_kernel(*refs):
    vs, ws, y_ref, pieces = refs[:NZ], refs[NZ : NZ + NX], refs[NZ + NX], refs[NZ + NX + 1 :]
    shots = vs[0].shape[0]
    total = dot_nt(block_of(vs, 0), ws[0][...])
    for k in range(1, NX):
        block = block_of(vs, k)
        pieces[-k][...] = block
        total += dot_nt(block, ws[k][...])
    total = total.astype(BF)
    for i in range(NZ):
        y_ref[back("z", i, NZ)] = total[i * shots : (i + 1) * shots]


def project(vs, ws):
    shots = vs[0].shape[0]
    return pl.pallas_call(
        project_kernel,
        name="project",
        out_shape=(shaped(NZ, shots, 4 * RANK),) + (shaped(NZ * shots, BLOCK),) * (NX - 1),
        in_specs=[VMEM_SPEC] * (NZ + NX),
        out_specs=(VMEM_SPEC,) * NX,
    )(vs[0], *near(*vs[1:]), ws[0], *near(*ws[1:]))


def total_kernel(part_ref, own_ref):
    own = part_ref[0].astype(F32)
    for i in range(1, NZ):
        own += part_ref[i].astype(F32)
    own_ref[...] = own.astype(BF)


def total(parts):
    return pl.pallas_call(
        total_kernel,
        name="total",
        out_shape=shaped(*parts.shape[1:]),
        in_specs=[VMEM_SPEC],
        out_specs=VMEM_SPEC,
    )(*near(parts))


def lowrank_kernel(g_ref, order_ref, *refs):
    ws, packs, (wf_ref, ws_ref, order_out) = refs[:NX], refs[NX : 2 * NX], refs[2 * NX :]
    order_out[...] = order_ref[...]
    p, s2, _, _, m2, m1 = (cols(g_ref[...], i) for i in range(6))
    mix = jnp.concatenate([m2, -(s2 + dot(p, m2)), -m1.T], axis=0)
    zero = jnp.zeros((RANK, BLOCK), BF)
    for k, (w, pack) in enumerate(zip(ws, packs)):
        left = w[0:64, :]
        right = pack[512:576, :]
        wf_ref[k, 0:64, :] = right
        wf_ref[k, 64:128, :] = zero
        wf_ref[k, 128:192, :] = (-(pack[576:640, :].astype(F32) + dot(p, right))).astype(BF)
        wf_ref[k, 192:256, :] = zero
        mixed = dot(mix, left)
        ws_ref[k, 0:64, :] = mixed[0:64].astype(BF)
        ws_ref[k, 64:128, :] = left
        ws_ref[k, 128:192, :] = mixed[64:128].astype(BF)
        ws_ref[k, 192:256, :] = (mixed[128:192] - w[128:192, :].astype(F32)).astype(BF)


def lowrank(g, order, ws, packs):
    return pl.pallas_call(
        lowrank_kernel,
        name="lowrank",
        out_shape=(shaped(NX, 4 * RANK, BLOCK),) * 2 + (shaped(*order.shape, dtype=jnp.int32),),
        in_specs=[VMEM_SPEC] * (2 + 2 * NX),
        out_specs=(VMEM_SPEC,) * 3,
    )(g, order, *ws, *packs)


def recur_kernel(f0, f1, f2, f3, g0, g1, g2, g3, out_ref, y_ref, g_ref):
    for k, f in enumerate((f0, f1, f2, f3)):
        y_ref[pl.ds(2 * k, 2)] = f[...]
    for k, g in enumerate((g0, g1, g2, g3)):
        g_ref[pl.ds(2 * k, 2)] = g[...]
    mine = lax.axis_index("leaf")
    core = lax.rem(mine, 2)
    line = lax.div(mine, 2)
    zero = jnp.zeros((f0.shape[1], RANK), F32)
    inc = inc_mine = zero
    steps, lifts = [], []
    for j in range(NLEAF):
        far = lax.rem(line + (NLEAF // 2 - j // 2), NLEAF // 2) * 2 + lax.rem(core + j, 2)
        maps = g_ref[far].astype(F32)
        p, s2, s1, s4, m2, m1 = (cols(maps, i) for i in range(6))
        y = y_ref[far].astype(F32)
        proj, y_q, y_carry, y_lift = (cols(y, i) for i in range(4))
        step = -(s1 + dot(p, m1))
        q_map = s2 + dot(p, m2)
        lift_map = s4 + dot_nt(p, s2)
        q = y_q + dot(proj, m2) - dot(inc, q_map)
        lift = y_lift + dot_nt(proj, s2) - dot(inc, lift_map) + dot_nt(q, p)
        inc_mine = jnp.where(mine == j, inc, inc_mine)
        inc = y_carry + dot(proj, m1) + dot(inc, step)
        steps.append(step)
        lifts.append(lift)
    ret = ret_mine = zero
    for j in range(NLEAF - 1, -1, -1):
        ret_mine = jnp.where(mine == j, ret, ret_mine)
        if j:
            ret = lifts[j] + dot_nt(ret, steps[j])
    late = jnp.concatenate([inc_mine, ret_mine], axis=1).astype(BF)
    for i in range(NZ):
        out_ref[i, :, 0:128] = y_ref[0, :, 0:128]
        out_ref[i, :, 128:256] = late


def recur(far, maps):
    return pl.pallas_call(
        recur_kernel,
        name="recur",
        out_shape=shaped(NZ, far[0].shape[1], 4 * RANK),
        in_specs=[VMEM_SPEC] * 8,
        out_specs=VMEM_SPEC,
        scratch_shapes=[pltpu.VMEM((NLEAF, *a[0].shape[1:]), BF) for a in (far, maps)],
    )(*near(*far, *maps))


def in_order(c_ref):
    return jnp.concatenate([c_ref[back("z", i, NZ)] for i in range(NZ)], axis=0)


def solve(v, coef, d, wf, ws):
    fwd = (dot(v, d) + dot(coef, wf)).astype(BF)
    return fwd, (dot_nt(fwd, d) + dot(coef, ws)).astype(BF)


def correlate_kernel(*refs):
    vs, packs = refs[:NZ], refs[NZ : NZ + NX]
    c_ref, wf_any, ws_any, sol_ref, cell_ref, v_ref, d_ref, wf_ref, ws_ref, sem = refs[NZ + NX :]
    waits = []
    for k in range(NX):
        moves = blocks_into(vs, k, v_ref)
        moves += [(packs[k], d_ref.at[k]), (wf_any.at[k], wf_ref.at[k]), (ws_any.at[k], ws_ref.at[k])]
        waits.append([pltpu.make_async_copy(a, b, sem.at[k, i]) for i, (a, b) in enumerate(moves)])
    for some in waits:
        for c in some:
            c.start()
    coef = in_order(c_ref)
    scale = 1.0 / jnp.sqrt(F32(NX * coef.shape[0]))
    high = lax.broadcasted_iota(jnp.int32, (cell_ref.shape[0], BLOCK), 0).astype(F32)
    low = lax.broadcasted_iota(jnp.int32, (LANES, BLOCK), 0).astype(F32)
    cells = None
    for k, some in enumerate(waits):
        for c in some:
            c.wait()
        fwd, sol = solve(v_ref[k], coef, d_ref[k, 0:512, :], wf_ref[k], ws_ref[k])
        if k == 0:
            sol_ref[...] = sol
        corr = jnp.sum(sol.astype(F32) * fwd.astype(F32), axis=0, keepdims=True) * scale
        cell = d_ref[k, 640:656, :].astype(F32)
        top = jnp.where(cell[8:9] >= LANES, 1.0, 0.0)
        at = jnp.where(high == cell[0:1] * 2.0 + top, 1.0, 0.0)
        part = dot_nt(at, jnp.where(low == cell[8:9] - top * LANES, corr, 0.0))
        cells = part if cells is None else cells + part
    cell_ref[...] = cells.astype(BF)


def correlate(vs, packs, coef, wf, ws):
    rows = NZ * vs[0].shape[0]
    return pl.pallas_call(
        correlate_kernel,
        name="correlate",
        out_shape=(shaped(rows, BLOCK), shaped(NZ * NX * SLAB // LANES, LANES)),
        in_specs=[ANY_SPEC] * (NZ + NX) + [VMEM_SPEC] + [ANY_SPEC] * 2,
        out_specs=(VMEM_SPEC,) * 2,
        scratch_shapes=[
            pltpu.VMEM((NX, rows, BLOCK), BF),
            pltpu.VMEM((NX, PACK, BLOCK), BF),
            pltpu.VMEM((NX, 4 * RANK, BLOCK), BF),
            pltpu.VMEM((NX, 4 * RANK, BLOCK), BF),
            pltpu.SemaphoreType.DMA((NX, NZ + 3)),
        ],
    )(*vs, *packs, *near(coef), wf, ws)


def others_kernel(*refs):
    count = NX - 1
    vs, coefs, (d_ref, wf_ref, ws_ref) = refs[:count], refs[count : 2 * count], refs[2 * count : -count]
    for v, c, sol in zip(vs, coefs, refs[-count:]):
        sol[...] = solve(v[...], in_order(c), d_ref[...], wf_ref[0], ws_ref[0])[1]


def others(vs, coefs, d, wf, ws):
    count = NX - 1
    return pl.pallas_call(
        others_kernel,
        name="others",
        out_shape=(shaped(*vs[0].shape),) * count,
        in_specs=[VMEM_SPEC] * (2 * count + 3),
        out_specs=(VMEM_SPEC,) * count,
    )(*vs, *near(*coefs), d, wf, ws)


def place_kernel(first, col_ref, *refs):
    pieces, out_ref = refs[:NX], refs[-1]
    tile = out_ref.shape[0]
    row = (pl.program_id(0) + first) * tile
    total = None
    for k, piece in enumerate(pieces):
        at = lax.broadcasted_iota(jnp.int32, (tile, piece.shape[0]), 0) + row
        part = dot(jnp.where(at == col_ref[k], 1.0, 0.0), piece[...])
        total = part if total is None else total + part
    out_ref[...] = total.astype(BF)


def place(columns, pieces, first, count, base=(), tile=512):
    return pl.pallas_call(
        functools.partial(place_kernel, first),
        name="place",
        grid=(count,),
        out_shape=shaped(NX * pieces[0].shape[0], BLOCK),
        in_specs=[VMEM_SPEC] * (1 + NX) + [ANY_SPEC] * len(base),
        out_specs=pl.BlockSpec((tile, BLOCK), lambda i: (i + first, 0)),
        input_output_aliases={1 + NX: 0} if base else {},
    )(columns, *pieces, *base)


def shifted(a, axis, by):
    count = lax.axis_size(axis)
    return lax.ppermute(a, axis, [(i, (i + by) % count) for i in range(count)])


def swapped(a, axis, bit):
    return lax.ppermute(a, axis, [(i, i ^ bit) for i in range(lax.axis_size(axis))])


def broadcast(a, axes):
    count = lax.axis_size(axes)
    return lax.all_to_all(jnp.broadcast_to(a[None], (count, *a.shape)), axes, 0, 0, tiled=True)


def around(a, axis):
    return [a] + [shifted(a, axis, k) for k in range(1, lax.axis_size(axis))]


def with_partners(a):
    a = jnp.stack([a, swapped(a, "leaf", 1)])
    return a


def over_lines(a):
    return [a] + [shifted(a, "leaf", 2 * k) for k in range(1, NLEAF // 2)]


def per_device(
    sources, block_inverse, basis_left, basis_right, couple_in, couple_out, column_of_shot, cell_map
):
    node = ("z", "x")
    shots = sources.shape[0]
    cells = cell_map.reshape(1, BLOCK)
    w, g, low, pack, *vs = prepare(
        sources, block_inverse, basis_left, basis_right, couple_in, couple_out, cells
    )
    for k in range(1, NZ):
        vs[k] = shifted(vs[k], "z", k)
    ws = around(w, "x")
    packs = around(pack, "x")
    for axis, bit in (("z", 1), ("z", 2), ("x", 1), ("x", 2), ("z", 4)):
        far = g if axis == "x" else low
        g = g + swapped(far, axis, bit).astype(F32)
        low = g.astype(BF)
    maps = with_partners(low)
    maps = over_lines(maps)
    z, x = lax.axis_index("z"), lax.axis_index("x")
    line = (z - jnp.arange(NZ)) % NZ * NX
    order = ((x - jnp.arange(NX))[:, None] % NX + line).reshape(-1)
    order = jnp.take(column_of_shot.reshape(NZ * NX, shots), order, axis=0, mode="clip")
    order = order.reshape(NX, 1, NZ * shots)
    wf, wb, order = lowrank(g, order, ws, packs)
    part, *pieces = project(vs, ws)
    parts = lax.all_to_all(part, "z", 0, 0, tiled=True)
    for k in range(1, NX):
        pieces[k - 1] = shifted(pieces[k - 1], "x", k)
    own = total(parts)
    pair = with_partners(own)
    far = over_lines(pair)
    coef = recur(far, maps)
    coef = lax.all_to_all(coef, "z", 0, 0, tiled=True)
    coefs = around(coef, "x")
    own, cells = correlate(vs, packs, coef, wf, wb)
    sols = others(pieces, coefs[1:], block_inverse, wf, wb)
    parts = cells.reshape(NZ * NX, SLAB // LANES, LANES)
    parts = lax.all_to_all(parts, node, 0, 0, tiled=True)
    slab = parts.astype(F32).sum(axis=0)
    gradient = broadcast(slab, "leaf").sum(axis=0).reshape(-1)
    placed = place(order, [own, *sols], 0, 2)
    solution = place(order, [own, *sols], 2, 2, (placed,))
    return solution, gradient


def solution(mesh):
    cut = Mesh(mesh.devices.reshape(NLEAF, NZ, NX), ("leaf", "z", "x"))
    block = P(None, ("leaf", "z", "x"))
    return jax.shard_map(
        per_device,
        mesh=cut,
        in_specs=(
            P(("z", "x"), "leaf"),
            block,
            block,
            block,
            block,
            block,
            P(),
            P(("leaf", "z", "x")),
        ),
        out_specs=(block, P(("z", "x"))),
        check_vma=False,
    )
```
